32 devices in a mesh: rep: 16 (over z, x, core), fsdp: 2 (over y).
Axes of the slice: x: 2, y: 2, z: 4, core: 2. Of those that a mesh axis runs over, the one named last changes fastest.
Arguments:
- gradients: bfloat16 [16, 4, 64, 4096], P('rep', None, 'fsdp'), may hold values from -8000 to 8000
- local_params: float32 [16, 4, 64, 4096], P('rep', None, 'fsdp'), may hold values from -6 to 6
- first_moment: float32 [16, 4, 64, 4096], P('rep', None, 'fsdp'), may hold values from -6 to 6
- second_moment: float32 [16, 4, 64, 4096], P('rep', None, 'fsdp'), may hold values from 0.05 to 2
- global_params: float32 [4, 64, 4096], P(None, 'fsdp'), may hold values from -6 to 6
- outer_momentum: float32 [4, 64, 4096], P(None, 'fsdp'), may hold values from -6 to 6
Outputs:
- new_global: float32 [4, 64, 4096], P(None, 'fsdp')
- new_momentum: float32 [4, 64, 4096], P(None, 'fsdp')
- new_first: float32 [16, 4, 64, 4096], P('rep', None, 'fsdp')
- new_second: float32 [16, 4, 64, 4096], P('rep', None, 'fsdp')
The draws below stay inside these ranges and needn't reach their ends.
All inputs are finite; a program needn't handle non-finite values.
Results may differ from the reference program's by a relative error of at most 0.0003.
Values sent between devices are 32-bit elements; how exact they have to be, the bound alone decides.
A program may use at most 128 MiB of HBM per device.

```python
import math
import jax
import jax.numpy as jnp
from jax import lax

D = 4096
MATRICES = 4
STEP = 20
ROWS = 64
REPLICAS = 16


def draw_gradients(key, part):
    keys = jax.random.split(key, 5)
    shape = (REPLICAS, MATRICES, ROWS, D)
    base = jnp.clip(jax.random.normal(keys[0], shape, jnp.float32), -6.0, 6.0)
    power = 1.0
    row_scale = jnp.exp(jax.random.uniform(keys[1], (REPLICAS, MATRICES, ROWS, 1), jnp.float32) * math.log(10.0))
    col_scale = jnp.exp(jax.random.uniform(keys[2], (REPLICAS, MATRICES, 1, D), jnp.float32) * math.log(10.0))
    ramp = 1.0 + 2.0 * jnp.arange(ROWS, dtype=jnp.float32) / max(ROWS - 1, 1)
    ramp = (ramp ** power).reshape(1, 1, ROWS, 1)
    values = base * row_scale * col_scale * ramp
    order = jax.random.permutation(keys[4], REPLICAS)
    quiet = (order < REPLICAS // 4).astype(jnp.float32).reshape(REPLICAS, 1, 1, 1)
    values = values * (1.0 - 0.999 * quiet)
    return jnp.clip(values, -8000.0, 8000.0).astype(jnp.bfloat16)


def block_levels(rng, shape, shards, low, largest):
    def one(axis_at, shards_of):
        steps = jax.random.uniform(jax.random.fold_in(jax.random.fold_in(rng, 6), axis_at), (shards_of,), jnp.float32, low / len(shards), largest / len(shards))
        return jnp.repeat(jnp.exp(steps), shape[axis_at] // shards_of).reshape((-1,) + (1,) * (len(shape) - axis_at - 1))

    level = one(*shards[0])
    for cut in shards[1:]:
        level = level * one(*cut)
    return level


def bell_draw(stream_key, dims, deviation, bound, cuts=(), kind=jnp.bfloat16):
    entries = jax.random.normal(stream_key, dims, jnp.float32) * deviation
    if len(cuts) > 0:
        entries = block_levels(stream_key, dims, cuts, -0.22, 0.18) * entries
    return jnp.clip(entries, min=-bound, max=bound).astype(kind)


def setup_inputs(seed: int = 0) -> dict:
    key_list = jax.random.split(jax.random.key(seed), 7)
    gradients = draw_gradients(jax.random.fold_in(key_list[6], 71), 0)
    local_params = bell_draw(key_list[1], (REPLICAS, MATRICES, ROWS, D), 1.0, 6.0, ((0, 16), (2, 2)), jnp.float32)
    first_moment = bell_draw(key_list[2], (REPLICAS, MATRICES, ROWS, D), 0.5, 6.0, ((0, 16), (2, 2)), jnp.float32)
    second_moment = jnp.clip(jnp.exp(math.log(2.0) - 3.6888794 * jax.random.uniform(key_list[3], (REPLICAS, MATRICES, ROWS, D), jnp.float32) ** block_levels(key_list[3], (REPLICAS, MATRICES, ROWS, D), ((0, 16), (2, 2)), -0.2, 0.2)), 0.05, 2.0)
    global_params = bell_draw(key_list[4], (MATRICES, ROWS, D), 1.0, 6.0, ((1, 2),), jnp.float32)
    outer_momentum = bell_draw(key_list[5], (MATRICES, ROWS, D), 0.5, 6.0, ((1, 2),), jnp.float32)
    return dict(gradients=gradients, local_params=local_params, first_moment=first_moment, second_moment=second_moment, global_params=global_params, outer_momentum=outer_momentum)


def reference(gradients, local_params, first_moment, second_moment, global_params, outer_momentum):
    first_fix = 1.0 - 0.9 ** STEP
    second_fix = 1.0 - 0.95 ** STEP

    def one_replica(carry, items):
        gradient, local_now, moment_one, moment_two = items
        gradient = gradient.astype(jnp.float32)
        squares = jnp.sum(gradient * gradient)
        rms_value = jnp.sqrt(squares / (MATRICES * ROWS * D))
        factor = jnp.minimum(1.0, 0.5 / rms_value)
        clipped = gradient * factor
        first_new = 0.9 * moment_one + 0.1 * clipped
        second_new = 0.95 * moment_two + 0.05 * clipped * clipped
        update = first_new / first_fix / (jnp.sqrt(second_new / second_fix) + 1e-08)
        stepped = local_now - 0.1 * (update + 0.1 * local_now)
        carry = carry + (global_params - stepped)
        return (carry, (first_new, second_new))
    start = jnp.zeros(global_params.shape, jnp.float32)
    total, (first_all, second_all) = lax.scan(one_replica, start, (gradients, local_params, first_moment, second_moment))
    pseudo = total / REPLICAS
    momentum_next = 0.9 * outer_momentum + pseudo
    global_next = global_params - 0.7 * (pseudo + 0.9 * momentum_next)
    return (global_next, momentum_next, first_all, second_all)
```

```python
import functools

import jax
import jax.numpy as jnp
from jax import lax
from jax.experimental import pallas as pl
from jax.experimental.pallas import tpu as pltpu
from jax.sharding import PartitionSpec as P

STEP = 20
FIRST_FIX = 1.0 - 0.9**STEP
SECOND_FIX = 1.0 - 0.95**STEP
CHUNKS = 16
HOP = 5
NEAR = 3
MESH = pl.DeviceIdType.MESH


def kernel(shape, g_hbm, p_hbm, f_hbm, s_hbm, w_hbm, v_hbm, new_w, new_v, new_f, new_s,
           g, p, f, s, w, v, delta, recv_c, part_x, recv_x, acc, recv_u, recv_m, res, squares,
           load_sem, sq_send, sq_recv, c_send, c_recv, x_send, x_recv, u_send, u_recv,
           m_send, m_recv, d_send, d_recv, b_send, b_recv, e_send, e_recv):
    reps, peers, depth = shape
    chunks, _, rows, width = delta.shape
    middle = depth // 2
    me = lax.axis_index("rep")
    fs = lax.axis_index("fsdp")
    core = lax.rem(me, 2)
    x = lax.rem(me // 2, 2)
    z = me // 4
    mine = 2 * core + x
    theirs = 2 * core + 1 - x
    left = jnp.where(z < middle, 1, 0)
    place = jnp.where(z < middle, z, depth - 1 - z)
    inward = 2 * left - 1
    other_core = {"rep": me + 1 - 2 * core}
    other_x = {"rep": me + 2 - 4 * x}
    inner = {"rep": me + 4 * inward}
    outer = {"rep": me - 4 * inward}
    at_end = place == 0
    at_middle = place == middle - 1

    loads = [pltpu.make_async_copy(src, dst, load_sem.at[i])
             for i, (src, dst) in enumerate(((g_hbm, g), (f_hbm, f), (s_hbm, s), (p_hbm, p), (w_hbm, w), (v_hbm, v)))]
    for load in loads:
        load.start()

    barrier = pltpu.get_barrier_semaphore()

    def greet(where):
        pl.semaphore_signal(barrier, inc=1, device_id=where, device_id_type=MESH)

    greet(other_core)
    greet(other_x)
    greet(inner)
    for d in range(1, peers):
        greet({"fsdp": lax.rem(fs + d, peers)})

    @pl.when(jnp.logical_not(at_end))
    def _():
        greet(outer)

    loads[0].wait()
    step = 512
    per = g.shape[2] // step

    def square(i, total):
        part = g[i // per, :, pl.ds(pl.multiple_of(lax.rem(i, per) * step, step), step)].astype(jnp.float32)
        return total + part * part

    sums = lax.fori_loop(0, g.shape[0] * per, square, jnp.zeros((rows, step), jnp.float32))
    sums = sum(sums[:, i * 128:(i + 1) * 128] for i in range(step // 128))
    squares[0] = sum(sums[i * 8:(i + 1) * 8] for i in range(rows // 8))

    pl.semaphore_wait(barrier, 3 + peers - 1 + jnp.where(at_end, 0, 1))

    sq = []
    for d in range(1, peers):
        copy = pltpu.make_async_remote_copy(
            squares.at[0], squares.at[d], sq_send.at[d], sq_recv.at[d],
            device_id={"fsdp": lax.rem(fs + d, peers)}, device_id_type=MESH)
        copy.start()
        sq.append(copy)
    for copy in sq:
        copy.wait()
    total = squares[0]
    for d in range(1, peers):
        total = total + squares[d]
    mean_sq = jnp.sum(total, keepdims=True) / (g.shape[0] * rows * g.shape[2] * peers)
    factor = jnp.where(mean_sq > 0.25, 0.5 / jnp.sqrt(mean_sq), 1.0)
    for load in loads[1:]:
        load.wait()

    def columns(k):
        return pl.ds(pl.multiple_of(k * width, width), width)

    def remote(src, dst, send, recv, where):
        return pltpu.make_async_remote_copy(src, dst, send, recv, device_id=where, device_id_type=MESH)

    def c_copy(k):
        return remote(delta.at[k, pl.ds(2 * (1 - core), 2)], recv_c.at[k], c_send.at[k], c_recv.at[k], other_core)

    def x_copy(k):
        return remote(part_x.at[k], recv_x.at[k], x_send.at[k], x_recv.at[k], other_x)

    def u_copy(k):
        return remote(acc.at[k], recv_u.at[k], u_send.at[k], u_recv.at[k], inner)

    def m_copy(k):
        return remote(acc.at[k], recv_m.at[k], m_send.at[k], m_recv.at[k], inner)

    def d_copy(k):
        return remote(res.at[k, mine], res.at[k, mine], d_send.at[k], d_recv.at[k], outer)

    def b_copy(k):
        return remote(res.at[k, mine], res.at[k, mine], b_send.at[k], b_recv.at[k], other_x)

    def e_copy(k, i, m):
        return remote(res.at[k, m], res.at[k, m], e_send.at[k, i], e_recv.at[k, i], other_core)

    def half(k, which):
        at = columns(k)
        for m in range(2):
            m = 2 * which + m
            clipped = g[m, :, at].astype(jnp.float32) * factor
            first = 0.9 * f[m, :, at] + 0.1 * clipped
            second = 0.95 * s[m, :, at] + 0.05 * clipped * clipped
            new_f[m, :, at] = first
            new_s[m, :, at] = second
            update = (first * (0.1 / FIRST_FIX)) / (jnp.sqrt(second * (1.0 / SECOND_FIX)) + 1e-8)
            delta[k, m] = 0.99 * p[m, :, at] - update

    def compute(k):
        half(k, 1 - core)
        c_copy(k).start()
        half(k, core)

    def reduce_core(k):
        c_copy(k).wait_recv()
        part_x[k] = delta[k, theirs] + recv_c[k, 1 - x]
        x_copy(k).start()

    def send_in(k):
        @pl.when(at_middle)
        def _():
            m_copy(k).start()

        @pl.when(jnp.logical_not(at_middle))
        def _():
            u_copy(k).start()

    def reduce_x(k):
        x_copy(k).wait_recv()
        acc[k] = delta[k, mine] + recv_c[k, x] + recv_x[k]

        @pl.when(at_end)
        def _():
            send_in(k)

    def reduce_z(k):
        @pl.when(jnp.logical_not(at_end))
        def _():
            u_copy(k).wait_recv()
            acc[k] = acc[k] + recv_u[k]
            send_in(k)

    def spread(k):
        @pl.when(at_middle)
        def _():
            m_copy(k).wait_recv()
            res[k, mine] = (acc[k] + recv_m[k]) * (1.0 / reps)

        @pl.when(jnp.logical_not(at_middle))
        def _():
            d_copy(k).wait_recv()

        b_copy(k).start()

        @pl.when(jnp.logical_not(at_end))
        def _():
            d_copy(k).start()

        e_copy(k, 0, mine).start()

    def gather_x(k):
        b_copy(k).wait_recv()
        e_copy(k, 1, theirs).start()

    def finish(k):
        e_copy(k, 0, mine).wait_recv()
        e_copy(k, 1, theirs).wait_recv()
        at = columns(k)
        for m in range(4):
            now = w[m, :, at]
            pseudo = now - res[k, m]
            momentum = 0.9 * v[m, :, at] + pseudo
            new_v[m, :, at] = momentum
            new_w[m, :, at] = now - 0.7 * (pseudo + 0.9 * momentum)

    def first_phase(t, _):
        @pl.when(t < chunks)
        def _():
            compute(t)

        @pl.when(t >= NEAR)
        def _():
            reduce_core(t - NEAR)
        return 0

    lax.fori_loop(0, chunks + NEAR, first_phase, 0)

    known = HOP * (2 * middle - 1 - place)
    stages = ((finish, known + HOP + NEAR), (gather_x, known + HOP), (spread, known), (reduce_z, HOP * place), (reduce_x, 0))

    def second_phase(t, _):
        for stage, lag in stages:
            @pl.when((t >= lag) & (t < lag + chunks))
            def _():
                stage(t - lag)
        return 0

    lax.fori_loop(0, chunks + HOP * 2 * middle + NEAR, second_phase, 0)

    def drain(k, _):
        c_copy(k).wait_send()
        x_copy(k).wait_send()
        b_copy(k).wait_send()
        e_copy(k, 0, mine).wait_send()
        e_copy(k, 1, theirs).wait_send()

        @pl.when(at_middle)
        def _():
            m_copy(k).wait_send()

        @pl.when(jnp.logical_not(at_middle))
        def _():
            u_copy(k).wait_send()

        @pl.when(jnp.logical_not(at_end))
        def _():
            d_copy(k).wait_send()
        return 0

    lax.fori_loop(0, chunks, drain, 0)


def store(*refs):
    half = len(refs) // 2
    sem = refs[-1]
    copies = [pltpu.make_async_copy(src, dst, sem.at[i]) for i, (src, dst) in enumerate(zip(refs[:half], refs[half:-1]))]
    for copy in copies:
        copy.start()
    for copy in copies:
        copy.wait()


def on_device(gradients, local_params, first_moment, second_moment, global_params, outer_momentum):
    reps, peers = lax.axis_size("rep"), lax.axis_size("fsdp")
    depth = reps // 4
    matrices, rows, d = global_params.shape
    width = d // CHUNKS
    f32 = jnp.float32
    piece = (rows, width)
    dma = pltpu.SemaphoreType.DMA
    block = (matrices, rows, d)
    results = pl.pallas_call(
        functools.partial(kernel, (reps, peers, depth)),
        out_shape=(pltpu.VMEM(block, f32),) * 4,
        in_specs=[pl.BlockSpec(memory_space=pltpu.HBM)] * 6,
        scratch_shapes=[
            pltpu.VMEM(block, gradients.dtype), *[pltpu.VMEM(block, f32)] * 5,
            pltpu.VMEM((CHUNKS, 4) + piece, f32),
            pltpu.VMEM((CHUNKS, 2) + piece, f32),
            *[pltpu.VMEM((CHUNKS,) + piece, f32)] * 5,
            pltpu.VMEM((CHUNKS, 4) + piece, f32),
            pltpu.VMEM((peers, 8, 128), f32),
            dma((6,)), dma((peers,)), dma((peers,)),
            *[dma((CHUNKS,))] * 12,
            *[dma((CHUNKS, 2))] * 2,
        ],
        compiler_params=pltpu.CompilerParams(
            collective_id=0, has_side_effects=True, vmem_limit_bytes=28 * 1024 * 1024),
    )(*[pltpu.with_memory_space_constraint(a.reshape(block), pltpu.HBM)
        for a in (gradients, local_params, first_moment, second_moment, global_params, outer_momentum)])
    outs = pl.pallas_call(
        store,
        out_shape=(jax.ShapeDtypeStruct(block, f32),) * 4,
        in_specs=[pl.BlockSpec(memory_space=pltpu.VMEM)] * 4,
        out_specs=(pl.BlockSpec(memory_space=pltpu.HBM),) * 4,
        scratch_shapes=[dma((4,))],
        compiler_params=pltpu.CompilerParams(vmem_limit_bytes=12 * 1024 * 1024),
    )(*results)
    return (outs[0], outs[1], outs[2][None], outs[3][None])


def solution(mesh):
    placed = (
        P("rep", None, "fsdp", None),
        P("rep", None, "fsdp", None),
        P("rep", None, "fsdp", None),
        P("rep", None, "fsdp", None),
        P(None, "fsdp", None),
        P(None, "fsdp", None),
    )
    return jax.shard_map(
        on_device,
        mesh=mesh,
        in_specs=placed,
        out_specs=(
            P(None, "fsdp", None),
            P(None, "fsdp", None),
            P("rep", None, "fsdp", None),
            P("rep", None, "fsdp", None),
        ),
        check_vma=False,
    )
```

```python
import functools

import jax
import jax.numpy as jnp
from jax import lax
from jax.experimental import pallas as pl
from jax.experimental.pallas import tpu as pltpu
from jax.sharding import PartitionSpec as P

STEP = 20
FIRST_FIX = 1.0 - 0.9**STEP
SECOND_FIX = 1.0 - 0.95**STEP
CHUNKS = 16
HOP = 5
NEAR = 3
MESH = pl.DeviceIdType.MESH


def kernel(shape, g_hbm, p_hbm, f_hbm, s_hbm, w_hbm, v_hbm, new_w, new_v, new_f, new_s,
           g, p, f, s, w, v, delta, recv_c, part_x, recv_x, acc, recv_u, recv_m, res, squares,
           load_sem, sq_send, sq_recv, c_send, c_recv, x_send, x_recv, u_send, u_recv,
           m_send, m_recv, d_send, d_recv, b_send, b_recv, e_send, e_recv):
    reps, peers, depth = shape
    chunks, _, rows, width = delta.shape
    middle = depth // 2
    me = lax.axis_index("rep")
    fs = lax.axis_index("fsdp")
    core = lax.rem(me, 2)
    x = lax.rem(me // 2, 2)
    z = me // 4
    mine = 2 * core + x
    theirs = 2 * core + 1 - x
    left = jnp.where(z < middle, 1, 0)
    place = jnp.where(z < middle, z, depth - 1 - z)
    inward = 2 * left - 1
    other_core = {"rep": me + 1 - 2 * core}
    other_x = {"rep": me + 2 - 4 * x}
    inner = {"rep": me + 4 * inward}
    outer = {"rep": me - 4 * inward}
    at_end = place == 0
    at_middle = place == middle - 1

    loads = [pltpu.make_async_copy(src, dst, load_sem.at[i])
             for i, (src, dst) in enumerate(((g_hbm, g), (f_hbm, f), (s_hbm, s), (p_hbm, p), (w_hbm, w), (v_hbm, v)))]
    for load in loads:
        load.start()

    barrier = pltpu.get_barrier_semaphore()

    def greet(where):
        pl.semaphore_signal(barrier, inc=1, device_id=where, device_id_type=MESH)

    greet(other_core)
    greet(other_x)
    greet(inner)
    for d in range(1, peers):
        greet({"fsdp": lax.rem(fs + d, peers)})

    @pl.when(jnp.logical_not(at_end))
    def _():
        greet(outer)

    loads[0].wait()
    step = 512
    per = g.shape[2] // step

    def square(i, total):
        part = g[i // per, :, pl.ds(pl.multiple_of(lax.rem(i, per) * step, step), step)].astype(jnp.float32)
        return total + part * part

    sums = lax.fori_loop(0, g.shape[0] * per, square, jnp.zeros((rows, step), jnp.float32))
    sums = sum(sums[:, i * 128:(i + 1) * 128] for i in range(step // 128))
    squares[0] = sum(sums[i * 8:(i + 1) * 8] for i in range(rows // 8))

    pl.semaphore_wait(barrier, 3 + peers - 1 + jnp.where(at_end, 0, 1))

    sq = []
    for d in range(1, peers):
        copy = pltpu.make_async_remote_copy(
            squares.at[0], squares.at[d], sq_send.at[d], sq_recv.at[d],
            device_id={"fsdp": lax.rem(fs + d, peers)}, device_id_type=MESH)
        copy.start()
        sq.append(copy)
    for copy in sq:
        copy.wait()
    total = squares[0]
    for d in range(1, peers):
        total = total + squares[d]
    mean_sq = jnp.sum(total, keepdims=True) / (g.shape[0] * rows * g.shape[2] * peers)
    factor = jnp.where(mean_sq > 0.25, 0.5 / jnp.sqrt(mean_sq), 1.0)
    for load in loads[1:4]:
        load.wait()

    def columns(k):
        return pl.ds(pl.multiple_of(k * width, width), width)

    def remote(src, dst, send, recv, where):
        return pltpu.make_async_remote_copy(src, dst, send, recv, device_id=where, device_id_type=MESH)

    def c_copy(k):
        return remote(delta.at[k, pl.ds(2 * (1 - core), 2)], recv_c.at[k], c_send.at[0], c_recv.at[k], other_core)

    def x_copy(k):
        return remote(part_x.at[k], recv_x.at[k], x_send.at[0], x_recv.at[k], other_x)

    def u_copy(k):
        return remote(acc.at[k], recv_u.at[k], u_send.at[0], u_recv.at[k], inner)

    def m_copy(k):
        return remote(acc.at[k], recv_m.at[k], m_send.at[0], m_recv.at[k], inner)

    def d_copy(k):
        return remote(res.at[k, mine], res.at[k, mine], d_send.at[0], d_recv.at[k], outer)

    def b_copy(k):
        return remote(res.at[k, mine], res.at[k, mine], b_send.at[0], b_recv.at[k], other_x)

    def e_copy(k):
        own = res.at[k, pl.ds(2 * core, 2)]
        return remote(own, own, e_send.at[0], e_recv.at[k], other_core)

    def half(k, which):
        at = columns(k)
        for m in range(2):
            m = 2 * which + m
            clipped = g[m, :, at].astype(jnp.float32) * factor
            first = 0.9 * f[m, :, at] + 0.1 * clipped
            second = 0.95 * s[m, :, at] + 0.05 * clipped * clipped
            new_f[m, :, at] = first
            new_s[m, :, at] = second
            update = (first * (0.1 / FIRST_FIX)) / (jnp.sqrt(second * (1.0 / SECOND_FIX)) + 1e-8)
            delta[k, m] = 0.99 * p[m, :, at] - update

    def compute(k):
        half(k, 1 - core)
        c_copy(k).start()
        half(k, core)

    def reduce_core(k):
        c_copy(k).wait_recv()
        part_x[k] = delta[k, theirs] + recv_c[k, 1 - x]
        x_copy(k).start()

    def send_in(k):
        @pl.when(at_middle)
        def _():
            m_copy(k).start()

        @pl.when(jnp.logical_not(at_middle))
        def _():
            u_copy(k).start()

    def reduce_x(k):
        x_copy(k).wait_recv()
        acc[k] = delta[k, mine] + recv_c[k, x] + recv_x[k]

        @pl.when(at_end)
        def _():
            send_in(k)

    def reduce_z(k):
        @pl.when(jnp.logical_not(at_end))
        def _():
            u_copy(k).wait_recv()
            acc[k] = acc[k] + recv_u[k]
            send_in(k)

    def spread(k):
        @pl.when(at_middle)
        def _():
            m_copy(k).wait_recv()
            res[k, mine] = (acc[k] + recv_m[k]) * (1.0 / reps)

        @pl.when(jnp.logical_not(at_middle))
        def _():
            d_copy(k).wait_recv()

        b_copy(k).start()

        @pl.when(jnp.logical_not(at_end))
        def _():
            d_copy(k).start()

    def gather_x(k):
        b_copy(k).wait_recv()
        e_copy(k).start()

    def finish(k):
        e_copy(k).wait_recv()
        at = columns(k)
        for m in range(4):
            now = w[m, :, at]
            pseudo = now - res[k, m]
            momentum = 0.9 * v[m, :, at] + pseudo
            new_v[m, :, at] = momentum
            new_w[m, :, at] = now - 0.7 * (pseudo + 0.9 * momentum)

    def first_phase(t, _):
        @pl.when(t < chunks)
        def _():
            compute(t)

        @pl.when(t >= NEAR)
        def _():
            reduce_core(t - NEAR)
        return 0

    lax.fori_loop(0, chunks + NEAR, first_phase, 0)

    for load in loads[4:]:
        load.wait()
    known = HOP * (2 * middle - 1 - place)
    stages = ((finish, known + HOP + NEAR), (gather_x, known + HOP), (spread, known), (reduce_z, HOP * place), (reduce_x, 0))

    def second_phase(t, _):
        for stage, lag in stages:
            @pl.when((t >= lag) & (t < lag + chunks))
            def _():
                stage(t - lag)
        return 0

    lax.fori_loop(0, chunks + HOP * 2 * middle + NEAR, second_phase, 0)

    def sent(like, sem):
        pltpu.make_async_copy(like, like, sem.at[0]).wait()

    sent(recv_c, c_send)
    sent(recv_x, x_send)
    sent(recv_x, b_send)
    sent(recv_c, e_send)

    @pl.when(at_middle)
    def _():
        sent(acc, m_send)

    @pl.when(jnp.logical_not(at_middle))
    def _():
        sent(acc, u_send)

    @pl.when(jnp.logical_not(at_end))
    def _():
        sent(acc, d_send)


def store(*refs):
    half = len(refs) // 2
    sem = refs[-1]
    copies = [pltpu.make_async_copy(src, dst, sem.at[i]) for i, (src, dst) in enumerate(zip(refs[:half], refs[half:-1]))]
    for copy in copies:
        copy.start()
    for copy in copies:
        copy.wait()


def on_device(gradients, local_params, first_moment, second_moment, global_params, outer_momentum):
    reps, peers = lax.axis_size("rep"), lax.axis_size("fsdp")
    depth = reps // 4
    matrices, rows, d = global_params.shape
    width = d // CHUNKS
    f32 = jnp.float32
    piece = (rows, width)
    dma = pltpu.SemaphoreType.DMA
    block = (matrices, rows, d)
    results = pl.pallas_call(
        functools.partial(kernel, (reps, peers, depth)),
        out_shape=(pltpu.VMEM(block, f32),) * 4,
        in_specs=[pl.BlockSpec(memory_space=pltpu.HBM)] * 6,
        scratch_shapes=[
            pltpu.VMEM(block, gradients.dtype), *[pltpu.VMEM(block, f32)] * 5,
            pltpu.VMEM((CHUNKS, 4) + piece, f32),
            pltpu.VMEM((CHUNKS, 2) + piece, f32),
            *[pltpu.VMEM((CHUNKS,) + piece, f32)] * 5,
            pltpu.VMEM((CHUNKS, 4) + piece, f32),
            pltpu.VMEM((peers, 8, 128), f32),
            dma((6,)), dma((peers,)), dma((peers,)),
            *[dma((1,)), dma((CHUNKS,))] * 7,
        ],
        compiler_params=pltpu.CompilerParams(
            collective_id=0, has_side_effects=True, vmem_limit_bytes=28 * 1024 * 1024),
    )(*[pltpu.with_memory_space_constraint(a.reshape(block), pltpu.HBM)
        for a in (gradients, local_params, first_moment, second_moment, global_params, outer_momentum)])
    outs = pl.pallas_call(
        store,
        out_shape=(jax.ShapeDtypeStruct(block, f32),) * 4,
        in_specs=[pl.BlockSpec(memory_space=pltpu.VMEM)] * 4,
        out_specs=(pl.BlockSpec(memory_space=pltpu.HBM),) * 4,
        scratch_shapes=[dma((4,))],
        compiler_params=pltpu.CompilerParams(vmem_limit_bytes=12 * 1024 * 1024),
    )(*results)
    return (outs[0], outs[1], outs[2][None], outs[3][None])


def solution(mesh):
    placed = (
        P("rep", None, "fsdp", None),
        P("rep", None, "fsdp", None),
        P("rep", None, "fsdp", None),
        P("rep", None, "fsdp", None),
        P(None, "fsdp", None),
        P(None, "fsdp", None),
    )
    return jax.shard_map(
        on_device,
        mesh=mesh,
        in_specs=placed,
        out_specs=(
            P(None, "fsdp", None),
            P(None, "fsdp", None),
            P("rep", None, "fsdp", None),
            P("rep", None, "fsdp", None),
        ),
        check_vma=False,
    )
```

```python
import functools

import jax
import jax.numpy as jnp
from jax import lax
from jax.experimental import pallas as pl
from jax.experimental.pallas import tpu as pltpu
from jax.sharding import PartitionSpec as P

STEP = 20
FIRST_FIX = 1.0 - 0.9**STEP
SECOND_FIX = 1.0 - 0.95**STEP
CHUNKS = 16
HOP = 5
STORES = 4
NEAR = 5
MESH = pl.DeviceIdType.MESH


def kernel(shape, g_hbm, p_hbm, f_hbm, s_hbm, w_hbm, v_hbm, res, w, v, new_f, new_s,
           g, p, f, s, delta, recv_c, part_x, recv_x, acc, recv_u, recv_m, squares,
           load_sem, sq_send, sq_recv, c_send, c_recv, x_send, x_recv, u_send, u_recv,
           m_send, m_recv, d_send, d_recv, b_send, b_recv, e_send, e_recv):
    reps, peers, depth = shape
    chunks, _, rows, width = delta.shape
    middle = depth // 2
    me = lax.axis_index("rep")
    fs = lax.axis_index("fsdp")
    core = lax.rem(me, 2)
    x = lax.rem(me // 2, 2)
    z = me // 4
    mine = 2 * core + x
    theirs = 2 * core + 1 - x
    left = jnp.where(z < middle, 1, 0)
    place = jnp.where(z < middle, z, depth - 1 - z)
    inward = 2 * left - 1
    other_core = {"rep": me + 1 - 2 * core}
    other_x = {"rep": me + 2 - 4 * x}
    inner = {"rep": me + 4 * inward}
    outer = {"rep": me - 4 * inward}
    at_end = place == 0
    at_middle = place == middle - 1

    loads = [pltpu.make_async_copy(src, dst, load_sem.at[i])
             for i, (src, dst) in enumerate(((g_hbm, g), (f_hbm, f), (s_hbm, s), (p_hbm, p), (w_hbm, w), (v_hbm, v)))]
    for load in loads:
        load.start()

    barrier = pltpu.get_barrier_semaphore()

    def greet(where):
        pl.semaphore_signal(barrier, inc=1, device_id=where, device_id_type=MESH)

    greet(other_core)
    greet(other_x)
    greet(inner)
    for d in range(1, peers):
        greet({"fsdp": lax.rem(fs + d, peers)})

    @pl.when(jnp.logical_not(at_end))
    def _():
        greet(outer)

    loads[0].wait()
    step = 512
    per = g.shape[2] // step

    def square(i, total):
        part = g[i // per, :, pl.ds(pl.multiple_of(lax.rem(i, per) * step, step), step)].astype(jnp.float32)
        return total + part * part

    sums = lax.fori_loop(0, g.shape[0] * per, square, jnp.zeros((rows, step), jnp.float32))
    sums = sum(sums[:, i * 128:(i + 1) * 128] for i in range(step // 128))
    squares[0] = sum(sums[i * 8:(i + 1) * 8] for i in range(rows // 8))

    pl.semaphore_wait(barrier, 3 + peers - 1 + jnp.where(at_end, 0, 1))

    sq = []
    for d in range(1, peers):
        copy = pltpu.make_async_remote_copy(
            squares.at[0], squares.at[d], sq_send.at[d], sq_recv.at[d],
            device_id={"fsdp": lax.rem(fs + d, peers)}, device_id_type=MESH)
        copy.start()
        sq.append(copy)
    for copy in sq:
        copy.wait()
    total = squares[0]
    for d in range(1, peers):
        total = total + squares[d]
    mean_sq = jnp.sum(total, keepdims=True) / (g.shape[0] * rows * g.shape[2] * peers)
    factor = jnp.where(mean_sq > 0.25, 0.5 / jnp.sqrt(mean_sq), 1.0)
    for load in loads[1:4]:
        load.wait()

    def columns(k):
        return pl.ds(pl.multiple_of(k * width, width), width)

    def remote(src, dst, send, recv, where):
        return pltpu.make_async_remote_copy(src, dst, send, recv, device_id=where, device_id_type=MESH)

    def c_copy(k):
        return remote(delta.at[k, pl.ds(2 * (1 - core), 2)], recv_c.at[k], c_send.at[0], c_recv.at[k], other_core)

    def x_copy(k):
        return remote(part_x.at[k], recv_x.at[k], x_send.at[0], x_recv.at[k], other_x)

    def u_copy(k):
        return remote(acc.at[k], recv_u.at[k], u_send.at[0], u_recv.at[k], inner)

    def m_copy(k):
        return remote(acc.at[k], recv_m.at[k], m_send.at[0], m_recv.at[k], inner)

    def d_copy(k):
        return remote(res.at[k, mine], res.at[k, mine], d_send.at[0], d_recv.at[k], outer)

    def b_copy(k):
        return remote(res.at[k, mine], res.at[k, mine], b_send.at[0], b_recv.at[k], other_x)

    def e_copy(k):
        own = res.at[k, pl.ds(2 * core, 2)]
        return remote(own, own, e_send.at[0], e_recv.at[0], other_core)

    def half(k, which):
        at = columns(k)
        for m in range(2):
            m = 2 * which + m
            clipped = g[m, :, at].astype(jnp.float32) * factor
            first = 0.9 * f[m, :, at] + 0.1 * clipped
            second = 0.95 * s[m, :, at] + 0.05 * clipped * clipped
            new_f[m, :, at] = first
            new_s[m, :, at] = second
            update = (first * (0.1 / FIRST_FIX)) / (jnp.sqrt(second * (1.0 / SECOND_FIX)) + 1e-8)
            delta[k, m] = 0.99 * p[m, :, at] - update

    def compute(k):
        half(k, 1 - core)
        c_copy(k).start()
        half(k, core)

    def reduce_core(k):
        c_copy(k).wait_recv()
        part_x[k] = delta[k, theirs] + recv_c[k, 1 - x]
        x_copy(k).start()

    def waits(role, kind, k):
        if kind == "x":
            x_copy(k).wait_recv()
        elif kind == "u":
            u_copy(k).wait_recv()
        elif kind == "known":
            (m_copy if role == middle - 1 else d_copy)(k).wait_recv()
        elif kind == "b":
            b_copy(k).wait_recv()

    def work(role, kind, k):
        if kind == "x":
            acc[k] = delta[k, mine] + recv_c[k, x] + recv_x[k]
        elif kind == "u":
            acc[k] = acc[k] + recv_u[k]
        elif kind == "known":
            if role == middle - 1:
                res[k, mine] = (acc[k] + recv_m[k]) * (1.0 / reps)

    def sends(role, kind, k):
        if kind == ("u" if role else "x"):
            (m_copy if role == middle - 1 else u_copy)(k).start()
        elif kind == "known":
            if role:
                d_copy(k).start()
            b_copy(k).start()
        elif kind == "b":
            e_copy(k).start()

    def first_phase(t, _):
        @pl.when(t < chunks)
        def _():
            compute(t)

        @pl.when(t >= NEAR)
        def _():
            reduce_core(t - NEAR)
        return 0

    lax.fori_loop(0, chunks + NEAR, first_phase, 0)

    def pipeline(role):
        known = HOP * (2 * middle - 1 - role)
        lags = {"x": 0, "u": HOP * role, "known": known, "b": known + HOP}
        if not role:
            del lags["u"]
        edges = sorted({lag + d for lag in lags.values() for d in (0, chunks)})
        for start, stop in zip(edges, edges[1:]):
            active = [(kind, lag) for kind, lag in lags.items() if lag <= start < lag + chunks]

            def body(t, _):
                for kind, lag in active:
                    for do in (waits, work, sends):
                        do(role, kind, t - lag)
                return 0

            if active:
                lax.fori_loop(start, stop, body, 0)

    for role in range(middle):
        @pl.when(place == role)
        def _():
            pipeline(role)

    def sent(like, sem):
        pltpu.make_async_copy(like, like, sem.at[0]).wait()

    sent(recv_c, c_send)
    sent(recv_x, x_send)
    sent(recv_x, b_send)
    sent(recv_c, e_send)
    sent(recv_c, e_recv)
    for load in loads[4:]:
        load.wait()

    @pl.when(at_middle)
    def _():
        sent(acc, m_send)

    @pl.when(jnp.logical_not(at_middle))
    def _():
        sent(acc, u_send)

    @pl.when(jnp.logical_not(at_end))
    def _():
        sent(acc, d_send)


def store(res, w, v, f, s, out_w, out_v, out_f, out_s, new_w, new_v, sem):
    copies = [pltpu.make_async_copy(src, dst, sem.at[i, 0]) for i, (src, dst) in enumerate(((f, out_f), (s, out_s)))]
    for copy in copies:
        copy.start()
    chunks, matrices, _, width = res.shape
    each = chunks // STORES
    for part in range(STORES):
        def piece(i, _):
            k, m = part * each + i // matrices, lax.rem(i, matrices)
            at = pl.ds(pl.multiple_of(k * width, width), width)
            now = w[m, :, at]
            pseudo = now - res[k, m]
            momentum = 0.9 * v[m, :, at] + pseudo
            new_v[m, :, at] = momentum
            new_w[m, :, at] = now - 0.7 * (pseudo + 0.9 * momentum)
            return 0

        lax.fori_loop(0, each * matrices, piece, 0)
        at = pl.ds(part * each * width, each * width)
        for i, (src, dst) in enumerate(((new_w, out_w), (new_v, out_v))):
            copies.append(pltpu.make_async_copy(src.at[:, :, at], dst.at[:, :, at], sem.at[i, 1 + part]))
            copies[-1].start()
    for copy in copies:
        copy.wait()


def on_device(gradients, local_params, first_moment, second_moment, global_params, outer_momentum):
    reps, peers = lax.axis_size("rep"), lax.axis_size("fsdp")
    depth = reps // 4
    matrices, rows, d = global_params.shape
    width = d // CHUNKS
    f32 = jnp.float32
    piece = (rows, width)
    dma = pltpu.SemaphoreType.DMA
    block = (matrices, rows, d)
    results = pl.pallas_call(
        functools.partial(kernel, (reps, peers, depth)),
        out_shape=(pltpu.VMEM((CHUNKS, matrices) + piece, f32), *[pltpu.VMEM(block, f32)] * 4),
        in_specs=[pl.BlockSpec(memory_space=pltpu.HBM)] * 6,
        scratch_shapes=[
            pltpu.VMEM(block, gradients.dtype), *[pltpu.VMEM(block, f32)] * 3,
            pltpu.VMEM((CHUNKS, 4) + piece, f32),
            pltpu.VMEM((CHUNKS, 2) + piece, f32),
            *[pltpu.VMEM((CHUNKS,) + piece, f32)] * 5,
            pltpu.VMEM((peers, 8, 128), f32),
            dma((6,)), dma((peers,)), dma((peers,)),
            *[dma((1,)), dma((CHUNKS,))] * 7,
        ],
        compiler_params=pltpu.CompilerParams(
            collective_id=0, has_side_effects=True, vmem_limit_bytes=28 * 1024 * 1024),
    )(*[pltpu.with_memory_space_constraint(a.reshape(block), pltpu.HBM)
        for a in (gradients, local_params, first_moment, second_moment, global_params, outer_momentum)])
    outs = pl.pallas_call(
        store,
        out_shape=(jax.ShapeDtypeStruct(block, f32),) * 4,
        in_specs=[pl.BlockSpec(memory_space=pltpu.VMEM)] * 5,
        out_specs=(pl.BlockSpec(memory_space=pltpu.HBM),) * 4,
        scratch_shapes=[*[pltpu.VMEM(block, f32)] * 2, dma((2, 1 + STORES))],
        compiler_params=pltpu.CompilerParams(vmem_limit_bytes=12 * 1024 * 1024),
    )(*results)
    return (outs[0], outs[1], outs[2][None], outs[3][None])


def solution(mesh):
    placed = (
        P("rep", None, "fsdp", None),
        P("rep", None, "fsdp", None),
        P("rep", None, "fsdp", None),
        P("rep", None, "fsdp", None),
        P(None, "fsdp", None),
        P(None, "fsdp", None),
    )
    return jax.shard_map(
        on_device,
        mesh=mesh,
        in_specs=placed,
        out_specs=(
            P(None, "fsdp", None),
            P(None, "fsdp", None),
            P("rep", None, "fsdp", None),
            P("rep", None, "fsdp", None),
        ),
        check_vma=False,
    )
```

```python
import functools

import jax
import jax.numpy as jnp
from jax import lax
from jax.experimental import pallas as pl
from jax.experimental.pallas import tpu as pltpu
from jax.sharding import PartitionSpec as P

STEP = 20
FIRST_FIX = 1.0 - 0.9**STEP
SECOND_FIX = 1.0 - 0.95**STEP
CHUNKS = 16
HOP = 5
STORES = 4
NEAR = 5
LINE = 2
OUT = 8
MESH = pl.DeviceIdType.MESH


def kernel(shape, g_hbm, p_hbm, f_hbm, s_hbm, w_hbm, v_hbm, res, w, v, new_f, new_s,
           g, p, f, s, delta, recv_c, part_x, recv_x, acc, recv_u, recv_m, squares,
           load_sem, sq_send, sq_recv, c_send, c_recv, x_send, x_recv, u_send, u_recv,
           m_send, m_recv, d_send, d_recv, b_send, b_recv, e_send, e_recv,
           line, recv_l, recv_h, own_h, recv_y, l_send, l_recv, h_send, h_recv, y_send, y_recv, g_send, g_recv, o_send, o_recv, o2_recv):
    reps, peers, depth = shape
    chunks, _, rows, width = delta.shape
    middle = depth // 2
    me = lax.axis_index("rep")
    fs = lax.axis_index("fsdp")
    core = lax.rem(me, 2)
    x = lax.rem(me // 2, 2)
    z = me // 4
    mine = 2 * core + x
    theirs = 2 * core + 1 - x
    left = jnp.where(z < middle, 1, 0)
    place = jnp.where(z < middle, z, depth - 1 - z)
    inward = 2 * left - 1
    other_core = {"rep": me + 1 - 2 * core}
    other_x = {"rep": me + 2 - 4 * x}
    inner = {"rep": me + 4 * inward}
    outer = {"rep": me - 4 * inward}
    keep = 1 - left
    ring = chunks - LINE
    at_end = place == 0
    at_middle = place == middle - 1

    loads = [pltpu.make_async_copy(src, dst, load_sem.at[i])
             for i, (src, dst) in enumerate(((g_hbm, g), (f_hbm, f), (s_hbm, s), (p_hbm, p), (w_hbm, w), (v_hbm, v)))]
    for load in loads:
        load.start()

    barrier = pltpu.get_barrier_semaphore()

    def greet(where):
        pl.semaphore_signal(barrier, inc=1, device_id=where, device_id_type=MESH)

    greet(other_core)
    greet(other_x)
    greet(inner)
    for d in range(1, peers):
        greet({"fsdp": lax.rem(fs + d, peers)})

    @pl.when(jnp.logical_not(at_end))
    def _():
        greet(outer)

    loads[0].wait()
    step = 512
    per = g.shape[2] // step

    def square(i, total):
        part = g[i // per, :, pl.ds(pl.multiple_of(lax.rem(i, per) * step, step), step)].astype(jnp.float32)
        return total + part * part

    sums = lax.fori_loop(0, g.shape[0] * per, square, jnp.zeros((rows, step), jnp.float32))
    sums = sum(sums[:, i * 128:(i + 1) * 128] for i in range(step // 128))
    squares[0] = sum(sums[i * 8:(i + 1) * 8] for i in range(rows // 8))

    pl.semaphore_wait(barrier, 3 + peers - 1 + jnp.where(at_end, 0, 1))

    sq = []
    for d in range(1, peers):
        copy = pltpu.make_async_remote_copy(
            squares.at[0], squares.at[d], sq_send.at[d], sq_recv.at[d],
            device_id={"fsdp": lax.rem(fs + d, peers)}, device_id_type=MESH)
        copy.start()
        sq.append(copy)
    for copy in sq:
        copy.wait()
    total = squares[0]
    for d in range(1, peers):
        total = total + squares[d]
    mean_sq = jnp.sum(total, keepdims=True) / (g.shape[0] * rows * g.shape[2] * peers)
    factor = jnp.where(mean_sq > 0.25, 0.5 / jnp.sqrt(mean_sq), 1.0)
    for load in loads[1:4]:
        load.wait()

    def columns(k):
        return pl.ds(pl.multiple_of(k * width, width), width)

    def remote(src, dst, send, recv, where):
        return pltpu.make_async_remote_copy(src, dst, send, recv, device_id=where, device_id_type=MESH)

    def c_copy(k):
        return remote(delta.at[k, pl.ds(2 * (1 - core), 2)], recv_c.at[k], c_send.at[0], c_recv.at[k], other_core)

    def x_copy(k):
        return remote(part_x.at[k], recv_x.at[k], x_send.at[0], x_recv.at[k], other_x)

    def u_copy(k):
        return remote(acc.at[k], recv_u.at[k], u_send.at[0], u_recv.at[k], inner)

    def m_copy(k):
        return remote(acc.at[k], recv_m.at[k], m_send.at[0], m_recv.at[k], inner)

    def d_copy(k):
        return remote(res.at[k, mine], res.at[k, mine], d_send.at[0], d_recv.at[k], outer)

    def b_copy(k):
        return remote(res.at[k, mine], res.at[k, mine], b_send.at[0], b_recv.at[k], other_x)

    def e_copy(k):
        own = res.at[k, pl.ds(2 * core, 2)]
        return remote(own, own, e_send.at[0], e_recv.at[0], other_core)

    def l_copy(j):
        return remote(line.at[j], recv_l.at[j], l_send.at[0], l_recv.at[j], inner)

    def h_copy(j):
        return remote(line.at[j, left], recv_h.at[j], h_send.at[0], h_recv.at[j], inner)

    def y_copy(j):
        return remote(own_h.at[j], recv_y.at[j], y_send.at[0], y_recv.at[j], other_x)

    def g_copy(j):
        at = res.at[ring + j, 2 * core + keep]
        return remote(at, at, g_send.at[0], g_recv.at[j], inner)

    def o_copy(j):
        at = res.at[ring + j, 2 * core + keep]
        return remote(at, at, o_send.at[0], o_recv.at[j], outer)

    def o2_copy(j):
        at = res.at[ring + j, 2 * core + left]
        return remote(at, at, o_send.at[0], o2_recv.at[j], outer)

    def half(k, which):
        at = columns(k)
        for m in range(2):
            m = 2 * which + m
            clipped = g[m, :, at].astype(jnp.float32) * factor
            first = 0.9 * f[m, :, at] + 0.1 * clipped
            second = 0.95 * s[m, :, at] + 0.05 * clipped * clipped
            new_f[m, :, at] = first
            new_s[m, :, at] = second
            update = (first * (0.1 / FIRST_FIX)) / (jnp.sqrt(second * (1.0 / SECOND_FIX)) + 1e-8)
            delta[k, m] = 0.99 * p[m, :, at] - update

    def compute(k):
        half(k, 1 - core)
        c_copy(k).start()
        half(k, core)

    def reduce_core(k):
        c_copy(k).wait_recv()
        part_x[k] = delta[k, theirs] + recv_c[k, 1 - x]
        x_copy(k).start()

    def waits(role, kind, k):
        if kind == "x":
            x_copy(k).wait_recv()
        elif kind == "u":
            u_copy(k).wait_recv()
        elif kind == "known":
            (m_copy if role == middle - 1 else d_copy)(k).wait_recv()
        elif kind == "b":
            b_copy(k).wait_recv()
        elif kind == "l":
            l_copy(k).wait_recv()
        elif kind == "h":
            h_copy(k).wait_recv()
        elif kind == "y":
            y_copy(k).wait_recv()
        elif kind == "g":
            g_copy(k).wait_recv()
        elif kind == "o":
            o_copy(k).wait_recv()
            o2_copy(k).wait_recv()

    def work(role, kind, k):
        if kind == "x":
            acc[k] = delta[k, mine] + recv_c[k, x] + recv_x[k]
        elif kind == "u":
            acc[k] = acc[k] + recv_u[k]
        elif kind == "known":
            if role == middle - 1:
                res[k, mine] = (acc[k] + recv_m[k]) * (1.0 / reps)

        elif kind == "l":
            line[k] = line[k] + recv_l[k]
        elif kind == "h":
            own_h[k] = line[k, keep] + recv_h[k]
        elif kind == "y":
            res[ring + k, 2 * core + keep] = (own_h[k] + recv_y[k]) * (1.0 / reps)

    def sends(role, kind, k):
        if kind == ("u" if role else "x"):
            (m_copy if role == middle - 1 else u_copy)(k).start()
        elif kind == "known":
            if role:
                d_copy(k).start()
            b_copy(k).start()
        elif kind == "b":
            e_copy(k).start()
        elif kind == "l":
            (h_copy if role == middle - 1 else l_copy)(k).start()
        elif kind == "h":
            y_copy(k).start()
        elif kind == "give":
            g_copy(k).start()
        elif kind == "out":
            o_copy(k).start()
        elif kind in ("g", "o"):
            if role:
                if kind == "o":
                    o_copy(k).start()
                o2_copy(k).start()
            e_copy(ring + k).start()

    def line_core(j):
        c_copy(ring + j).wait_recv()
        line[j] = delta[ring + j, pl.ds(2 * core, 2)] + recv_c[ring + j]

        @pl.when(at_end)
        def _():
            l_copy(j).start()

    order = [0, 1] + [ring + j for j in range(LINE)] + list(range(2, ring))
    whole = LINE + 2 + NEAR

    for k in order[:NEAR]:
        compute(k)
    for t in range(NEAR, whole):
        compute(order[t])
        k = order[t - NEAR]
        if k < ring:
            reduce_core(k)
        else:
            line_core(k - ring)

    def first_phase(t, _):
        compute(t)
        reduce_core(t - NEAR)
        return 0

    lax.fori_loop(whole - LINE, ring, first_phase, 0)

    def last_cores(t, _):
        reduce_core(t)
        return 0

    lax.fori_loop(ring - NEAR, ring, last_cores, 0)

    def pipeline(role):
        known = HOP * (2 * middle - 1 - role)
        stages = [("x", 0, 0, ring)]
        if role:
            stages.append(("u", HOP * role, 0, ring))
        stages += [("known", known, 0, ring), ("b", known + HOP, 0, ring)]
        if role:
            stages.append(("l", 3 + HOP * (role - 1), 0, LINE))
        out = HOP * middle + ring
        if role == middle - 1:
            half_at = 3 + HOP * role
            across = max(half_at + HOP, ring + 1)
            give = max(across + 1, ring + HOP * role)
            stages += [("h", half_at, 0, LINE), ("y", across, 0, LINE), ("give", give, 0, LINE),
                       ("out", out, 0, LINE), ("g", out + 1, 0, LINE)]
        else:
            stages.append(("o", out + OUT + HOP * (middle - 2 - role), 0, LINE))
        edges = sorted({lag + k for _, lag, low, high in stages for k in (low, high)})
        for start, stop in zip(edges, edges[1:]):
            active = [(kind, lag) for kind, lag, low, high in stages if lag + low <= start < lag + high]

            def body(t, _):
                for kind, lag in active:
                    for do in (waits, work, sends):
                        do(role, kind, t - lag)
                return 0

            if active:
                lax.fori_loop(start, stop, body, 0)

    for role in range(middle):
        @pl.when(place == role)
        def _():
            pipeline(role)

    def sent(like, sem):
        pltpu.make_async_copy(like, like, sem.at[0]).wait()

    sent(recv_c, c_send)
    sent(recv_x, x_send)
    sent(recv_x, b_send)
    sent(recv_c, e_send)
    sent(recv_c, e_recv)
    for load in loads[4:]:
        load.wait()

    @pl.when(at_middle)
    def _():
        sent(acc, m_send)
        sent(recv_h, h_send)
        sent(recv_y, y_send)
        sent(recv_h, g_send)

    @pl.when(jnp.logical_not(at_middle))
    def _():
        sent(acc, u_send)
        sent(recv_l, l_send)

    @pl.when(jnp.logical_not(at_end))
    def _():
        sent(acc, d_send)
        sent(recv_l, o_send)


def store(res, w, v, f, s, out_w, out_v, out_f, out_s, new_w, new_v, sem):
    copies = [pltpu.make_async_copy(src, dst, sem.at[i, 0]) for i, (src, dst) in enumerate(((f, out_f), (s, out_s)))]
    for copy in copies:
        copy.start()
    chunks, matrices, _, width = res.shape
    each = chunks // STORES
    for part in range(STORES):
        def piece(i, _):
            k, m = part * each + i // matrices, lax.rem(i, matrices)
            at = pl.ds(pl.multiple_of(k * width, width), width)
            now = w[m, :, at]
            pseudo = now - res[k, m]
            momentum = 0.9 * v[m, :, at] + pseudo
            new_v[m, :, at] = momentum
            new_w[m, :, at] = now - 0.7 * (pseudo + 0.9 * momentum)
            return 0

        lax.fori_loop(0, each * matrices, piece, 0)
        at = pl.ds(part * each * width, each * width)
        for i, (src, dst) in enumerate(((new_w, out_w), (new_v, out_v))):
            copies.append(pltpu.make_async_copy(src.at[:, :, at], dst.at[:, :, at], sem.at[i, 1 + part]))
            copies[-1].start()
    for copy in copies:
        copy.wait()


def on_device(gradients, local_params, first_moment, second_moment, global_params, outer_momentum):
    reps, peers = lax.axis_size("rep"), lax.axis_size("fsdp")
    depth = reps // 4
    matrices, rows, d = global_params.shape
    width = d // CHUNKS
    f32 = jnp.float32
    piece = (rows, width)
    dma = pltpu.SemaphoreType.DMA
    block = (matrices, rows, d)
    results = pl.pallas_call(
        functools.partial(kernel, (reps, peers, depth)),
        out_shape=(pltpu.VMEM((CHUNKS, matrices) + piece, f32), *[pltpu.VMEM(block, f32)] * 4),
        in_specs=[pl.BlockSpec(memory_space=pltpu.HBM)] * 6,
        scratch_shapes=[
            pltpu.VMEM(block, gradients.dtype), *[pltpu.VMEM(block, f32)] * 3,
            pltpu.VMEM((CHUNKS, 4) + piece, f32),
            pltpu.VMEM((CHUNKS, 2) + piece, f32),
            *[pltpu.VMEM((CHUNKS - LINE,) + piece, f32)] * 5,
            pltpu.VMEM((peers, 8, 128), f32),
            dma((6,)), dma((peers,)), dma((peers,)),
            *[dma((1,)), dma((CHUNKS,))] * 7,
            *[pltpu.VMEM((LINE, 2) + piece, f32)] * 2,
            *[pltpu.VMEM((LINE,) + piece, f32)] * 3,
            *[dma((1,)), dma((LINE,))] * 5, dma((LINE,)),
        ],
        compiler_params=pltpu.CompilerParams(
            collective_id=0, has_side_effects=True, vmem_limit_bytes=28 * 1024 * 1024),
    )(*[pltpu.with_memory_space_constraint(a.reshape(block), pltpu.HBM)
        for a in (gradients, local_params, first_moment, second_moment, global_params, outer_momentum)])
    outs = pl.pallas_call(
        store,
        out_shape=(jax.ShapeDtypeStruct(block, f32),) * 4,
        in_specs=[pl.BlockSpec(memory_space=pltpu.VMEM)] * 5,
        out_specs=(pl.BlockSpec(memory_space=pltpu.HBM),) * 4,
        scratch_shapes=[*[pltpu.VMEM(block, f32)] * 2, dma((2, 1 + STORES))],
        compiler_params=pltpu.CompilerParams(vmem_limit_bytes=12 * 1024 * 1024),
    )(*results)
    return (outs[0], outs[1], outs[2][None], outs[3][None])


def solution(mesh):
    placed = (
        P("rep", None, "fsdp", None),
        P("rep", None, "fsdp", None),
        P("rep", None, "fsdp", None),
        P("rep", None, "fsdp", None),
        P(None, "fsdp", None),
        P(None, "fsdp", None),
    )
    return jax.shard_map(
        on_device,
        mesh=mesh,
        in_specs=placed,
        out_specs=(
            P(None, "fsdp", None),
            P(None, "fsdp", None),
            P("rep", None, "fsdp", None),
            P("rep", None, "fsdp", None),
        ),
        check_vma=False,
    )
```

```python
import functools

import jax
import jax.numpy as jnp
from jax import lax
from jax.experimental import pallas as pl
from jax.experimental.pallas import tpu as pltpu
from jax.sharding import PartitionSpec as P

STEP = 20
FIRST_FIX = 1.0 - 0.9**STEP
SECOND_FIX = 1.0 - 0.95**STEP
CHUNKS = 16
HOP = 5
STORES = 4
NEAR = 5
LINE = 1
OUT = 8
MESH = pl.DeviceIdType.MESH


def kernel(shape, g_hbm, p_hbm, f_hbm, s_hbm, w_hbm, v_hbm, res, w, v, new_f, new_s,
           g, p, f, s, delta, recv_c, part_x, recv_x, acc, recv_u, recv_m, squares,
           load_sem, sq_send, sq_recv, c_send, c_recv, x_send, x_recv, u_send, u_recv,
           m_send, m_recv, d_send, d_recv, b_send, b_recv, e_send, e_recv,
           line, recv_l, recv_h, own_h, recv_y, l_send, l_recv, h_send, h_recv, y_send, y_recv, g_send, g_recv, o_send, o_recv, o2_recv):
    reps, peers, depth = shape
    chunks, _, rows, width = delta.shape
    middle = depth // 2
    me = lax.axis_index("rep")
    fs = lax.axis_index("fsdp")
    core = lax.rem(me, 2)
    x = lax.rem(me // 2, 2)
    z = me // 4
    mine = 2 * core + x
    theirs = 2 * core + 1 - x
    left = jnp.where(z < middle, 1, 0)
    place = jnp.where(z < middle, z, depth - 1 - z)
    inward = 2 * left - 1
    other_core = {"rep": me + 1 - 2 * core}
    other_x = {"rep": me + 2 - 4 * x}
    inner = {"rep": me + 4 * inward}
    outer = {"rep": me - 4 * inward}
    keep = 1 - left
    ring = chunks - LINE
    at_end = place == 0
    at_middle = place == middle - 1

    loads = [pltpu.make_async_copy(src, dst, load_sem.at[i])
             for i, (src, dst) in enumerate(((g_hbm, g), (f_hbm, f), (s_hbm, s), (p_hbm, p), (w_hbm, w), (v_hbm, v)))]
    for load in loads:
        load.start()

    barrier = pltpu.get_barrier_semaphore()

    def greet(where):
        pl.semaphore_signal(barrier, inc=1, device_id=where, device_id_type=MESH)

    greet(other_core)
    greet(other_x)
    greet(inner)
    for d in range(1, peers):
        greet({"fsdp": lax.rem(fs + d, peers)})

    @pl.when(jnp.logical_not(at_end))
    def _():
        greet(outer)

    loads[0].wait()
    step = 512
    per = g.shape[2] // step

    def square(i, total):
        part = g[i // per, :, pl.ds(pl.multiple_of(lax.rem(i, per) * step, step), step)].astype(jnp.float32)
        return total + part * part

    sums = lax.fori_loop(0, g.shape[0] * per, square, jnp.zeros((rows, step), jnp.float32))
    sums = sum(sums[:, i * 128:(i + 1) * 128] for i in range(step // 128))
    squares[0] = sum(sums[i * 8:(i + 1) * 8] for i in range(rows // 8))

    pl.semaphore_wait(barrier, 3 + peers - 1 + jnp.where(at_end, 0, 1))

    sq = []
    for d in range(1, peers):
        copy = pltpu.make_async_remote_copy(
            squares.at[0], squares.at[d], sq_send.at[d], sq_recv.at[d],
            device_id={"fsdp": lax.rem(fs + d, peers)}, device_id_type=MESH)
        copy.start()
        sq.append(copy)
    for copy in sq:
        copy.wait()
    total = squares[0]
    for d in range(1, peers):
        total = total + squares[d]
    mean_sq = jnp.sum(total, keepdims=True) / (g.shape[0] * rows * g.shape[2] * peers)
    factor = jnp.where(mean_sq > 0.25, 0.5 / jnp.sqrt(mean_sq), 1.0)
    for load in loads[1:4]:
        load.wait()

    def columns(k):
        return pl.ds(pl.multiple_of(k * width, width), width)

    def remote(src, dst, send, recv, where):
        return pltpu.make_async_remote_copy(src, dst, send, recv, device_id=where, device_id_type=MESH)

    def c_copy(k):
        return remote(delta.at[k, pl.ds(2 * (1 - core), 2)], recv_c.at[k], c_send.at[0], c_recv.at[k], other_core)

    def x_copy(k):
        return remote(part_x.at[k], recv_x.at[k], x_send.at[0], x_recv.at[k], other_x)

    def u_copy(k):
        return remote(acc.at[k], recv_u.at[k], u_send.at[0], u_recv.at[k], inner)

    def m_copy(k):
        return remote(acc.at[k], recv_m.at[k], m_send.at[0], m_recv.at[k], inner)

    def d_copy(k):
        return remote(res.at[k, mine], res.at[k, mine], d_send.at[0], d_recv.at[k], outer)

    def b_copy(k):
        return remote(res.at[k, mine], res.at[k, mine], b_send.at[0], b_recv.at[k], other_x)

    def e_copy(k):
        own = res.at[k, pl.ds(2 * core, 2)]
        return remote(own, own, e_send.at[0], e_recv.at[0], other_core)

    def l_copy(j):
        return remote(line.at[j], recv_l.at[j], l_send.at[0], l_recv.at[j], inner)

    def h_copy(j):
        return remote(line.at[j, left], recv_h.at[j], h_send.at[0], h_recv.at[j], inner)

    def y_copy(j):
        return remote(own_h.at[j], recv_y.at[j], y_send.at[0], y_recv.at[j], other_x)

    def g_copy(j):
        at = res.at[ring + j, 2 * core + keep]
        return remote(at, at, g_send.at[0], g_recv.at[j], inner)

    def o_copy(j):
        at = res.at[ring + j, 2 * core + keep]
        return remote(at, at, o_send.at[0], o_recv.at[j], outer)

    def o2_copy(j):
        at = res.at[ring + j, 2 * core + left]
        return remote(at, at, o_send.at[0], o2_recv.at[j], outer)

    def half(k, which):
        at = columns(k)
        for m in range(2):
            m = 2 * which + m
            clipped = g[m, :, at].astype(jnp.float32) * factor
            first = 0.9 * f[m, :, at] + 0.1 * clipped
            second = 0.95 * s[m, :, at] + 0.05 * clipped * clipped
            new_f[m, :, at] = first
            new_s[m, :, at] = second
            update = (first * (0.1 / FIRST_FIX)) / (jnp.sqrt(second * (1.0 / SECOND_FIX)) + 1e-8)
            delta[k, m] = 0.99 * p[m, :, at] - update

    def compute(k):
        half(k, 1 - core)
        c_copy(k).start()
        half(k, core)

    def reduce_core(k):
        c_copy(k).wait_recv()
        part_x[k] = delta[k, theirs] + recv_c[k, 1 - x]
        x_copy(k).start()

    def waits(role, kind, k):
        if kind == "x":
            x_copy(k).wait_recv()
        elif kind == "u":
            u_copy(k).wait_recv()
        elif kind == "known":
            (m_copy if role == middle - 1 else d_copy)(k).wait_recv()
        elif kind == "b":
            b_copy(k).wait_recv()
        elif kind == "l":
            l_copy(k).wait_recv()
        elif kind == "h":
            h_copy(k).wait_recv()
        elif kind == "y":
            y_copy(k).wait_recv()
        elif kind == "g":
            g_copy(k).wait_recv()
        elif kind == "o":
            o_copy(k).wait_recv()
            o2_copy(k).wait_recv()

    def work(role, kind, k):
        if kind == "x":
            acc[k] = delta[k, mine] + recv_c[k, x] + recv_x[k]
        elif kind == "u":
            acc[k] = acc[k] + recv_u[k]
        elif kind == "known":
            if role == middle - 1:
                res[k, mine] = (acc[k] + recv_m[k]) * (1.0 / reps)

        elif kind == "l":
            line[k] = line[k] + recv_l[k]
        elif kind == "h":
            own_h[k] = line[k, keep] + recv_h[k]
        elif kind == "y":
            res[ring + k, 2 * core + keep] = (own_h[k] + recv_y[k]) * (1.0 / reps)

    def sends(role, kind, k):
        if kind == ("u" if role else "x"):
            (m_copy if role == middle - 1 else u_copy)(k).start()
        elif kind == "known":
            if role:
                d_copy(k).start()
            b_copy(k).start()
        elif kind == "b":
            e_copy(k).start()
        elif kind == "l":
            (h_copy if role == middle - 1 else l_copy)(k).start()
        elif kind == "h":
            y_copy(k).start()
        elif kind == "give":
            g_copy(k).start()
        elif kind == "out":
            o_copy(k).start()
        elif kind in ("g", "o"):
            if role:
                if kind == "o":
                    o_copy(k).start()
                o2_copy(k).start()
            e_copy(ring + k).start()

    def line_core(j):
        c_copy(ring + j).wait_recv()
        line[j] = delta[ring + j, pl.ds(2 * core, 2)] + recv_c[ring + j]

        @pl.when(at_end)
        def _():
            l_copy(j).start()

    order = [0, 1] + [ring + j for j in range(LINE)] + list(range(2, ring))
    whole = LINE + 2 + NEAR

    for k in order[:NEAR]:
        compute(k)
    for t in range(NEAR, whole):
        compute(order[t])
        k = order[t - NEAR]
        if k < ring:
            reduce_core(k)
        else:
            line_core(k - ring)

    def first_phase(t, _):
        compute(t)
        reduce_core(t - NEAR)
        return 0

    lax.fori_loop(whole - LINE, ring, first_phase, 0)

    def last_cores(t, _):
        reduce_core(t)
        return 0

    lax.fori_loop(ring - NEAR, ring, last_cores, 0)

    def pipeline(role):
        known = HOP * (2 * middle - 1 - role)
        stages = [("x", 0, 0, ring)]
        if role:
            stages.append(("u", HOP * role - 1, 0, ring))
        stages += [("known", known, 0, ring), ("b", known + HOP, 0, ring)]
        if role:
            stages.append(("l", 3 + HOP * (role - 1), 0, LINE))
        out = HOP * middle + ring
        if role == middle - 1:
            half_at = 3 + HOP * role
            across = max(half_at + HOP, ring + 1)
            give = max(across + 1, ring + HOP * role)
            stages += [("h", half_at, 0, LINE), ("y", across, 0, LINE), ("give", give, 0, LINE),
                       ("out", out, 0, LINE), ("g", out + 1, 0, LINE)]
        else:
            stages.append(("o", out + OUT + HOP * (middle - 2 - role), 0, LINE))
        edges = sorted({lag + k for _, lag, low, high in stages for k in (low, high)})
        for start, stop in zip(edges, edges[1:]):
            active = [(kind, lag) for kind, lag, low, high in stages if lag + low <= start < lag + high]

            def body(t, _):
                for kind, lag in active:
                    for do in (waits, work, sends):
                        do(role, kind, t - lag)
                return 0

            if active:
                lax.fori_loop(start, stop, body, 0)

    for role in range(middle):
        @pl.when(place == role)
        def _():
            pipeline(role)

    def sent(like, sem):
        pltpu.make_async_copy(like, like, sem.at[0]).wait()

    sent(recv_c, c_send)
    sent(recv_x, x_send)
    sent(recv_x, b_send)
    sent(recv_c, e_send)
    sent(recv_c, e_recv)
    for load in loads[4:]:
        load.wait()

    @pl.when(at_middle)
    def _():
        sent(acc, m_send)
        sent(recv_h, h_send)
        sent(recv_y, y_send)
        sent(recv_h, g_send)

    @pl.when(jnp.logical_not(at_middle))
    def _():
        sent(acc, u_send)
        sent(recv_l, l_send)

    @pl.when(jnp.logical_not(at_end))
    def _():
        sent(acc, d_send)
        sent(recv_l, o_send)


def store(res, w, v, f, s, out_w, out_v, out_f, out_s, new_w, new_v, sem):
    copies = [pltpu.make_async_copy(src, dst, sem.at[i, 0]) for i, (src, dst) in enumerate(((f, out_f), (s, out_s)))]
    for copy in copies:
        copy.start()
    chunks, matrices, _, width = res.shape
    each = chunks // STORES
    for part in range(STORES):
        def piece(i, _):
            k, m = part * each + i // matrices, lax.rem(i, matrices)
            at = pl.ds(pl.multiple_of(k * width, width), width)
            now = w[m, :, at]
            pseudo = now - res[k, m]
            momentum = 0.9 * v[m, :, at] + pseudo
            new_v[m, :, at] = momentum
            new_w[m, :, at] = now - 0.7 * (pseudo + 0.9 * momentum)
            return 0

        lax.fori_loop(0, each * matrices, piece, 0)
        at = pl.ds(part * each * width, each * width)
        for i, (src, dst) in enumerate(((new_w, out_w), (new_v, out_v))):
            copies.append(pltpu.make_async_copy(src.at[:, :, at], dst.at[:, :, at], sem.at[i, 1 + part]))
            copies[-1].start()
    for copy in copies:
        copy.wait()


def on_device(gradients, local_params, first_moment, second_moment, global_params, outer_momentum):
    reps, peers = lax.axis_size("rep"), lax.axis_size("fsdp")
    depth = reps // 4
    matrices, rows, d = global_params.shape
    width = d // CHUNKS
    f32 = jnp.float32
    piece = (rows, width)
    dma = pltpu.SemaphoreType.DMA
    block = (matrices, rows, d)
    results = pl.pallas_call(
        functools.partial(kernel, (reps, peers, depth)),
        out_shape=(pltpu.VMEM((CHUNKS, matrices) + piece, f32), *[pltpu.VMEM(block, f32)] * 4),
        in_specs=[pl.BlockSpec(memory_space=pltpu.HBM)] * 6,
        scratch_shapes=[
            pltpu.VMEM(block, gradients.dtype), *[pltpu.VMEM(block, f32)] * 3,
            pltpu.VMEM((CHUNKS, 4) + piece, f32),
            pltpu.VMEM((CHUNKS, 2) + piece, f32),
            *[pltpu.VMEM((CHUNKS - LINE,) + piece, f32)] * 5,
            pltpu.VMEM((peers, 8, 128), f32),
            dma((6,)), dma((peers,)), dma((peers,)),
            *[dma((1,)), dma((CHUNKS,))] * 7,
            *[pltpu.VMEM((LINE, 2) + piece, f32)] * 2,
            *[pltpu.VMEM((LINE,) + piece, f32)] * 3,
            *[dma((1,)), dma((LINE,))] * 5, dma((LINE,)),
        ],
        compiler_params=pltpu.CompilerParams(
            collective_id=0, has_side_effects=True, vmem_limit_bytes=28 * 1024 * 1024),
    )(*[pltpu.with_memory_space_constraint(a.reshape(block), pltpu.HBM)
        for a in (gradients, local_params, first_moment, second_moment, global_params, outer_momentum)])
    outs = pl.pallas_call(
        store,
        out_shape=(jax.ShapeDtypeStruct(block, f32),) * 4,
        in_specs=[pl.BlockSpec(memory_space=pltpu.VMEM)] * 5,
        out_specs=(pl.BlockSpec(memory_space=pltpu.HBM),) * 4,
        scratch_shapes=[*[pltpu.VMEM(block, f32)] * 2, dma((2, 1 + STORES))],
        compiler_params=pltpu.CompilerParams(vmem_limit_bytes=12 * 1024 * 1024),
    )(*results)
    return (outs[0], outs[1], outs[2][None], outs[3][None])


def solution(mesh):
    placed = (
        P("rep", None, "fsdp", None),
        P("rep", None, "fsdp", None),
        P("rep", None, "fsdp", None),
        P("rep", None, "fsdp", None),
        P(None, "fsdp", None),
        P(None, "fsdp", None),
    )
    return jax.shard_map(
        on_device,
        mesh=mesh,
        in_specs=placed,
        out_specs=(
            P(None, "fsdp", None),
            P(None, "fsdp", None),
            P("rep", None, "fsdp", None),
            P("rep", None, "fsdp", None),
        ),
        check_vma=False,
    )
```

```python
import functools

import jax
import jax.numpy as jnp
from jax import lax
from jax.experimental import pallas as pl
from jax.experimental.pallas import tpu as pltpu
from jax.sharding import PartitionSpec as P

STEP = 20
FIRST_FIX = 1.0 - 0.9**STEP
SECOND_FIX = 1.0 - 0.95**STEP
CHUNKS = 16
HOP = 5
STORES = 4
NEAR = 5
LINE = 1
OUT = 8
MESH = pl.DeviceIdType.MESH


def kernel(shape, g_hbm, p_hbm, f_hbm, s_hbm, w_hbm, v_hbm, res, w, v, new_f, new_s,
           g, p, f, s, delta, recv_c, part_x, recv_x, acc, recv_u, recv_m, squares,
           load_sem, sq_send, sq_recv, c_send, c_recv, x_send, x_recv, u_send, u_recv,
           m_send, m_recv, d_send, d_recv, b_send, b_recv, e_send, e_recv,
           line, recv_l, recv_h, own_h, recv_y, l_send, l_recv, h_send, h_recv, y_send, y_recv, g_send, g_recv, o_send, o_recv, o2_recv):
    reps, peers, depth = shape
    chunks, _, rows, width = delta.shape
    middle = depth // 2
    me = lax.axis_index("rep")
    fs = lax.axis_index("fsdp")
    core = lax.rem(me, 2)
    x = lax.rem(me // 2, 2)
    z = me // 4
    mine = 2 * core + x
    theirs = 2 * core + 1 - x
    left = jnp.where(z < middle, 1, 0)
    place = jnp.where(z < middle, z, depth - 1 - z)
    inward = 2 * left - 1
    other_core = {"rep": me + 1 - 2 * core}
    other_x = {"rep": me + 2 - 4 * x}
    inner = {"rep": me + 4 * inward}
    outer = {"rep": me - 4 * inward}
    keep = 1 - left
    ring = chunks - LINE
    at_end = place == 0
    at_middle = place == middle - 1

    loads = [pltpu.make_async_copy(src, dst, load_sem.at[i])
             for i, (src, dst) in enumerate(((g_hbm, g), (f_hbm, f), (s_hbm, s), (p_hbm, p), (w_hbm, w), (v_hbm, v)))]
    for load in loads:
        load.start()

    barrier = pltpu.get_barrier_semaphore()

    def greet(where):
        pl.semaphore_signal(barrier, inc=1, device_id=where, device_id_type=MESH)

    greet(other_core)
    greet(other_x)
    greet(inner)
    for d in range(1, peers):
        greet({"fsdp": lax.rem(fs + d, peers)})

    @pl.when(jnp.logical_not(at_end))
    def _():
        greet(outer)

    loads[0].wait()
    step = 512
    per = g.shape[2] // step

    def square(i, total):
        part = g[i // per, :, pl.ds(pl.multiple_of(lax.rem(i, per) * step, step), step)].astype(jnp.float32)
        return total + part * part

    sums = lax.fori_loop(0, g.shape[0] * per, square, jnp.zeros((rows, step), jnp.float32))
    sums = sum(sums[:, i * 128:(i + 1) * 128] for i in range(step // 128))
    sums = sum(sums[i * 8:(i + 1) * 8] for i in range(rows // 8))
    squares[0] = jnp.broadcast_to(jnp.sum(sums, keepdims=True), (8, 128))

    pl.semaphore_wait(barrier, 3 + peers - 1 + jnp.where(at_end, 0, 1))

    sq = []
    for d in range(1, peers):
        copy = pltpu.make_async_remote_copy(
            squares.at[0], squares.at[d], sq_send.at[d], sq_recv.at[d],
            device_id={"fsdp": lax.rem(fs + d, peers)}, device_id_type=MESH)
        copy.start()
        sq.append(copy)
    for copy in sq:
        copy.wait()
    total = squares[0]
    for d in range(1, peers):
        total = total + squares[d]
    mean_sq = total[:1, :1] / (g.shape[0] * rows * g.shape[2] * peers)
    factor = jnp.where(mean_sq > 0.25, 0.5 / jnp.sqrt(mean_sq), 1.0)
    for load in loads[1:4]:
        load.wait()

    def columns(k):
        return pl.ds(pl.multiple_of(k * width, width), width)

    def remote(src, dst, send, recv, where):
        return pltpu.make_async_remote_copy(src, dst, send, recv, device_id=where, device_id_type=MESH)

    def c_copy(k):
        return remote(delta.at[k, pl.ds(2 * (1 - core), 2)], recv_c.at[k], c_send.at[0], c_recv.at[k], other_core)

    def x_copy(k):
        return remote(part_x.at[k], recv_x.at[k], x_send.at[0], x_recv.at[k], other_x)

    def u_copy(k):
        return remote(acc.at[k], recv_u.at[k], u_send.at[0], u_recv.at[k], inner)

    def m_copy(k):
        return remote(acc.at[k], recv_m.at[k], m_send.at[0], m_recv.at[k], inner)

    def d_copy(k):
        return remote(res.at[k, mine], res.at[k, mine], d_send.at[0], d_recv.at[k], outer)

    def b_copy(k):
        return remote(res.at[k, mine], res.at[k, mine], b_send.at[0], b_recv.at[k], other_x)

    def e_copy(k):
        own = res.at[k, pl.ds(2 * core, 2)]
        return remote(own, own, e_send.at[0], e_recv.at[0], other_core)

    def l_copy(j):
        return remote(line.at[j], recv_l.at[j], l_send.at[0], l_recv.at[j], inner)

    def h_copy(j):
        return remote(line.at[j, left], recv_h.at[j], h_send.at[0], h_recv.at[j], inner)

    def y_copy(j):
        return remote(own_h.at[j], recv_y.at[j], y_send.at[0], y_recv.at[j], other_x)

    def g_copy(j):
        at = res.at[ring + j, 2 * core + keep]
        return remote(at, at, g_send.at[0], g_recv.at[j], inner)

    def o_copy(j):
        at = res.at[ring + j, 2 * core + keep]
        return remote(at, at, o_send.at[0], o_recv.at[j], outer)

    def o2_copy(j):
        at = res.at[ring + j, 2 * core + left]
        return remote(at, at, o_send.at[0], o2_recv.at[j], outer)

    def half(k, which):
        at = columns(k)
        for m in range(2):
            m = 2 * which + m
            clipped = g[m, :, at].astype(jnp.float32) * factor
            first = 0.9 * f[m, :, at] + 0.1 * clipped
            second = 0.95 * s[m, :, at] + 0.05 * clipped * clipped
            new_f[m, :, at] = first
            new_s[m, :, at] = second
            update = (first * (0.1 / FIRST_FIX)) / (jnp.sqrt(second * (1.0 / SECOND_FIX)) + 1e-8)
            delta[k, m] = 0.99 * p[m, :, at] - update

    def compute(k):
        half(k, 1 - core)
        c_copy(k).start()
        half(k, core)

    def reduce_core(k):
        c_copy(k).wait_recv()
        part_x[k] = delta[k, theirs] + recv_c[k, 1 - x]
        x_copy(k).start()
        acc[k] = delta[k, mine] + recv_c[k, x]

    def waits(role, kind, k):
        if kind == "x":
            x_copy(k).wait_recv()
        elif kind == "u":
            u_copy(k).wait_recv()
        elif kind == "known":
            (m_copy if role == middle - 1 else d_copy)(k).wait_recv()
        elif kind == "b":
            b_copy(k).wait_recv()
        elif kind == "l":
            l_copy(k).wait_recv()
        elif kind == "h":
            h_copy(k).wait_recv()
        elif kind == "y":
            y_copy(k).wait_recv()
        elif kind == "g":
            g_copy(k).wait_recv()
        elif kind == "o":
            o_copy(k).wait_recv()
            o2_copy(k).wait_recv()

    def work(role, kind, k):
        if kind == "x":
            acc[k] = acc[k] + recv_x[k]
        elif kind == "u":
            acc[k] = acc[k] + recv_u[k]
        elif kind == "known":
            if role == middle - 1:
                res[k, mine] = (acc[k] + recv_m[k]) * (1.0 / reps)

        elif kind == "l":
            line[k] = line[k] + recv_l[k]
        elif kind == "h":
            own_h[k] = line[k, keep] + recv_h[k]
        elif kind == "y":
            res[ring + k, 2 * core + keep] = (own_h[k] + recv_y[k]) * (1.0 / reps)

    def sends(role, kind, k):
        if kind == ("u" if role else "x"):
            (m_copy if role == middle - 1 else u_copy)(k).start()
        elif kind == "known":
            if role:
                d_copy(k).start()
            b_copy(k).start()
        elif kind == "b":
            e_copy(k).start()
        elif kind == "l":
            (h_copy if role == middle - 1 else l_copy)(k).start()
        elif kind == "h":
            y_copy(k).start()
        elif kind == "give":
            g_copy(k).start()
        elif kind == "out":
            o_copy(k).start()
        elif kind in ("g", "o"):
            if role:
                if kind == "o":
                    o_copy(k).start()
                o2_copy(k).start()
            e_copy(ring + k).start()

    def line_core(j):
        c_copy(ring + j).wait_recv()
        line[j] = delta[ring + j, pl.ds(2 * core, 2)] + recv_c[ring + j]

        @pl.when(at_end)
        def _():
            l_copy(j).start()

    order = [0, 1] + [ring + j for j in range(LINE)] + list(range(2, ring))
    whole = LINE + 2 + NEAR

    for k in order[:NEAR]:
        compute(k)
    for t in range(NEAR, whole):
        compute(order[t])
        k = order[t - NEAR]
        if k < ring:
            reduce_core(k)
        else:
            line_core(k - ring)

    def first_phase(t, _):
        compute(t)
        reduce_core(t - NEAR)
        return 0

    lax.fori_loop(whole - LINE, ring, first_phase, 0)

    def last_cores(t, _):
        reduce_core(t)
        return 0

    lax.fori_loop(ring - NEAR, ring, last_cores, 0)

    def pipeline(role):
        known = HOP * (2 * middle - 1 - role)
        stages = [("x", 0, 0, ring)]
        if role:
            stages.append(("u", HOP * role - 1, 0, ring))
        stages += [("known", known, 0, ring), ("b", known + HOP, 0, ring)]
        if role:
            stages.append(("l", 3 + HOP * (role - 1), 0, LINE))
        out = HOP * middle + ring
        if role == middle - 1:
            half_at = 3 + HOP * role
            across = max(half_at + HOP, ring + 1)
            give = max(across + 1, ring + HOP * role)
            stages += [("h", half_at, 0, LINE), ("y", across, 0, LINE), ("give", give, 0, LINE),
                       ("out", out, 0, LINE), ("g", out + 1, 0, LINE)]
        else:
            stages.append(("o", out + OUT + HOP * (middle - 2 - role), 0, LINE))
        edges = sorted({lag + k for _, lag, low, high in stages for k in (low, high)})
        for start, stop in zip(edges, edges[1:]):
            active = [(kind, lag) for kind, lag, low, high in stages if lag + low <= start < lag + high]

            def body(t, _):
                for kind, lag in active:
                    for do in (waits, work, sends):
                        do(role, kind, t - lag)
                return 0

            if active:
                lax.fori_loop(start, stop, body, 0)

    for role in range(middle):
        @pl.when(place == role)
        def _():
            pipeline(role)

    def sent(like, sem):
        pltpu.make_async_copy(like, like, sem.at[0]).wait()

    sent(recv_c, c_send)
    sent(recv_x, x_send)
    sent(recv_x, b_send)
    sent(recv_c, e_send)
    sent(recv_c, e_recv)
    for load in loads[4:]:
        load.wait()

    @pl.when(at_middle)
    def _():
        sent(acc, m_send)
        sent(recv_h, h_send)
        sent(recv_y, y_send)
        sent(recv_h, g_send)

    @pl.when(jnp.logical_not(at_middle))
    def _():
        sent(acc, u_send)
        sent(recv_l, l_send)

    @pl.when(jnp.logical_not(at_end))
    def _():
        sent(acc, d_send)
        sent(recv_l, o_send)


def store(res, w, v, f, s, out_w, out_v, out_f, out_s, new_w, new_v, sem):
    copies = [pltpu.make_async_copy(src, dst, sem.at[i, 0]) for i, (src, dst) in enumerate(((f, out_f), (s, out_s)))]
    for copy in copies:
        copy.start()
    chunks, matrices, _, width = res.shape
    each = chunks // STORES
    for part in range(STORES):
        def piece(i, _):
            k, m = part * each + i // matrices, lax.rem(i, matrices)
            at = pl.ds(pl.multiple_of(k * width, width), width)
            now = w[m, :, at]
            pseudo = now - res[k, m]
            momentum = 0.9 * v[m, :, at] + pseudo
            new_v[m, :, at] = momentum
            new_w[m, :, at] = now - 0.7 * (pseudo + 0.9 * momentum)
            return 0

        lax.fori_loop(0, each * matrices, piece, 0)
        at = pl.ds(part * each * width, each * width)
        for i, (src, dst) in enumerate(((new_w, out_w), (new_v, out_v))):
            copies.append(pltpu.make_async_copy(src.at[:, :, at], dst.at[:, :, at], sem.at[i, 1 + part]))
            copies[-1].start()
    for copy in copies:
        copy.wait()


def on_device(gradients, local_params, first_moment, second_moment, global_params, outer_momentum):
    reps, peers = lax.axis_size("rep"), lax.axis_size("fsdp")
    depth = reps // 4
    matrices, rows, d = global_params.shape
    width = d // CHUNKS
    f32 = jnp.float32
    piece = (rows, width)
    dma = pltpu.SemaphoreType.DMA
    block = (matrices, rows, d)
    results = pl.pallas_call(
        functools.partial(kernel, (reps, peers, depth)),
        out_shape=(pltpu.VMEM((CHUNKS, matrices) + piece, f32), *[pltpu.VMEM(block, f32)] * 4),
        in_specs=[pl.BlockSpec(memory_space=pltpu.HBM)] * 6,
        scratch_shapes=[
            pltpu.VMEM(block, gradients.dtype), *[pltpu.VMEM(block, f32)] * 3,
            pltpu.VMEM((CHUNKS, 4) + piece, f32),
            pltpu.VMEM((CHUNKS, 2) + piece, f32),
            *[pltpu.VMEM((CHUNKS - LINE,) + piece, f32)] * 5,
            pltpu.VMEM((peers, 8, 128), f32),
            dma((6,)), dma((peers,)), dma((peers,)),
            *[dma((1,)), dma((CHUNKS,))] * 7,
            *[pltpu.VMEM((LINE, 2) + piece, f32)] * 2,
            *[pltpu.VMEM((LINE,) + piece, f32)] * 3,
            *[dma((1,)), dma((LINE,))] * 5, dma((LINE,)),
        ],
        compiler_params=pltpu.CompilerParams(
            collective_id=0, has_side_effects=True, vmem_limit_bytes=28 * 1024 * 1024),
    )(*[pltpu.with_memory_space_constraint(a.reshape(block), pltpu.HBM)
        for a in (gradients, local_params, first_moment, second_moment, global_params, outer_momentum)])
    outs = pl.pallas_call(
        store,
        out_shape=(jax.ShapeDtypeStruct(block, f32),) * 4,
        in_specs=[pl.BlockSpec(memory_space=pltpu.VMEM)] * 5,
        out_specs=(pl.BlockSpec(memory_space=pltpu.HBM),) * 4,
        scratch_shapes=[*[pltpu.VMEM(block, f32)] * 2, dma((2, 1 + STORES))],
        compiler_params=pltpu.CompilerParams(vmem_limit_bytes=12 * 1024 * 1024),
    )(*results)
    return (outs[0], outs[1], outs[2][None], outs[3][None])


def solution(mesh):
    placed = (
        P("rep", None, "fsdp", None),
        P("rep", None, "fsdp", None),
        P("rep", None, "fsdp", None),
        P("rep", None, "fsdp", None),
        P(None, "fsdp", None),
        P(None, "fsdp", None),
    )
    return jax.shard_map(
        on_device,
        mesh=mesh,
        in_specs=placed,
        out_specs=(
            P(None, "fsdp", None),
            P(None, "fsdp", None),
            P("rep", None, "fsdp", None),
            P("rep", None, "fsdp", None),
        ),
        check_vma=False,
    )
```
